256 devices in a mesh: row: 16 (over z_lo, y, core), col: 16 (over z_hi, x).
Axes of the slice: x: 4, y: 4, z: 8 (z_hi: 4, z_lo: 2; z = z_hi * 2 + z_lo), core: 2. Of those that a mesh axis runs over, the one named last changes fastest.
Arguments:
- page_scores: bfloat16 [393216, 128], P('row'), may hold values from -6 to 6
- tile_values: bfloat16 [16, 16, 22, 512, 512], P('row', 'col'), may hold values from -0.25 to 0.25
- tile_row: int32 [16, 16, 22], P('row', 'col'), may hold values from 0 to 47, as said below
- tile_col: int32 [16, 16, 22], P('row', 'col'), may hold values from 0 to 7, as said below
- tile_count: int32 [16, 16], P('row', 'col'), may hold values from 2 to 22, as said below
- page_seed: int32 [393216], P(('row', 'col')), may hold values 0 or 1
- page_label: int32 [393216], P(('row', 'col')), may hold values from 0 to 127
- page_degree: int32 [393216], P(('row', 'col')), may hold values from 4 to 64
- feature_seed: int32 [65536], P('col'), may hold values 0 or 1
- feature_label: int32 [65536], P('col'), may hold values from 0 to 127
- feature_degree: int32 [65536], P('col'), may hold values from 4 to 64
Outputs:
- new_page_scores: bfloat16 [393216, 128], P(('row', 'col'))
The draws below stay inside these ranges and needn't reach their ends.
Inputs may be any that keep to these rules, and one draw needn't show every extreme that they name: `tile_row`: within each grid cell the first tile_count slots name distinct tile positions; later slots are unused. `tile_col`: paired with tile_row slot by slot. `tile_count`: some grid cell has all 22 slots live in every draw.
All inputs are finite; a program needn't handle non-finite values. No bound on the sum of `page_seed` or of `feature_seed` on one device may be relied on, other than what follows from the above.
Results may differ from the reference program's by a relative error of at most 0.0047.
Values may be sent and summed in bfloat16 or wider, within the bound.
No kernel may reach another device: no remote copies, remote signals or barrier semaphores. Data moves between devices by JAX's collectives and lax.ppermute only.
A program may use at most 128 MiB of HBM per device.

```python
import jax
import jax.numpy as jnp
from jax import lax

C = 128
TILE = 512
P_BLK = 24576
F_BLK = 4096
TILES = 22
PAGES = 393216
FEATS = 65536
N_ROW = 16
N_COL = 16


def tile_layout(key):
    base = jax.random.fold_in(key, 11)
    ndevices = N_ROW * N_COL
    across = F_BLK // TILE
    slots = P_BLK // TILE * across

    def shuffle_slots(single_key):
        return jax.random.permutation(single_key, slots)
    keys = jax.random.split(jax.random.fold_in(base, 1), ndevices)
    order = jax.vmap(shuffle_slots)(keys)[:, :TILES].astype(jnp.int32)
    rows = (order // across).reshape(N_ROW, N_COL, TILES)
    cols = (order % across).reshape(N_ROW, N_COL, TILES)
    lower = jax.random.randint(jax.random.fold_in(base, 2), (ndevices,), 2, TILES // 2 + 1, dtype=jnp.int32)
    heavy = jax.random.randint(jax.random.fold_in(base, 3), (ndevices,), 0, 8, dtype=jnp.int32) == 0
    forced = jax.random.randint(jax.random.fold_in(base, 4), (), 0, ndevices, dtype=jnp.int32)
    full = heavy | (jnp.arange(ndevices, dtype=jnp.int32) == forced)
    counts = jnp.where(full, TILES, lower).astype(jnp.int32).reshape(N_ROW, N_COL)
    return (rows, cols, counts)


def draw_tile_row(key, part):
    return tile_layout(key)[0]


def draw_tile_col(key, part):
    return tile_layout(key)[1]


def draw_tile_count(key, part):
    return tile_layout(key)[2]


def plant(entries, stream_key, least, largest):
    spot = [jax.random.randint(jax.random.fold_in(stream_key, axis), (), 0, length) for axis, length in enumerate(entries.shape)]
    main_axis = entries.shape.index(max(entries.shape))
    beside = spot[:main_axis] + [(spot[main_axis] + 1) % entries.shape[main_axis]] + spot[main_axis + 1:]
    return entries.at[tuple(spot)].set(least).at[tuple(beside)].set(largest)


def steps_of(stream_key, extent, cuts, smallest, top_value):
    level, own = 1.0, jax.random.fold_in(stream_key, 6)
    for axis_at, blocks in cuts:
        draws = jnp.exp(jax.random.uniform(jax.random.fold_in(own, axis_at), (blocks,), jnp.float32, smallest / len(cuts), top_value / len(cuts)))
        level = level * jnp.repeat(draws, extent[axis_at] // blocks).reshape([-1 if axis == axis_at else 1 for axis in range(len(extent))])
    return level


def centred(own_key, shape, width, limit, pieces=(), held_as=jnp.bfloat16):
    values = width * jax.random.normal(own_key, shape, jnp.float32)
    if pieces:
        values = values * steps_of(own_key, shape, pieces, -0.22, 0.18)
    return jnp.clip(values, -limit, limit).astype(held_as)


def setup_inputs(seed: int = 0) -> dict:
    splits = jax.random.split(jax.random.key(seed), 12)
    page_scores = centred(splits[0], (PAGES, C), 1.0, 6.0, ((0, 16),))
    tile_values = centred(splits[1], (N_ROW, N_COL, TILES, TILE, TILE), TILE ** -0.5, 0.25, ((0, 16), (1, 16)))
    tile_row = draw_tile_row(jax.random.fold_in(splits[11], 71), 0)
    tile_col = draw_tile_col(jax.random.fold_in(splits[11], 71), 0)
    tile_count = draw_tile_count(jax.random.fold_in(splits[11], 71), 0)
    page_seed = plant((jax.random.randint(splits[5], (PAGES,), 0, 8) < 1).astype(jnp.int32), jax.random.fold_in(splits[5], 1), 0, 1)
    page_label = plant(jax.random.randint(splits[6], (PAGES,), 0, C), jax.random.fold_in(splits[6], 1), 0, C - 1).astype(jnp.int32)
    page_degree = plant(jax.random.randint(splits[7], (PAGES,), 4, 65), jax.random.fold_in(splits[7], 1), 4, 64).astype(jnp.int32)
    feature_seed = plant((jax.random.randint(splits[8], (FEATS,), 0, 8) < 1).astype(jnp.int32), jax.random.fold_in(splits[8], 1), 0, 1)
    feature_label = plant(jax.random.randint(splits[9], (FEATS,), 0, C), jax.random.fold_in(splits[9], 1), 0, C - 1).astype(jnp.int32)
    feature_degree = plant(jax.random.randint(splits[10], (FEATS,), 4, 65), jax.random.fold_in(splits[10], 1), 4, 64).astype(jnp.int32)
    return dict(page_scores=page_scores, tile_values=tile_values, tile_row=tile_row, tile_col=tile_col, tile_count=tile_count, page_seed=page_seed, page_label=page_label, page_degree=page_degree, feature_seed=feature_seed, feature_label=feature_label, feature_degree=feature_degree)


def clamp_scores(sums, degree, known, label):
    classes = lax.broadcasted_iota(jnp.int32, sums.shape, 1)
    hot = (label[:, None] == classes).astype(jnp.float32)
    scaled = sums * lax.rsqrt(degree.astype(jnp.float32))[:, None]
    return jnp.where(known[:, None] == 1, hot, scaled)

def reference(page_scores, tile_values, tile_row, tile_col, tile_count, page_seed, page_label, page_degree, feature_seed, feature_label, feature_degree):
    ndevices = N_ROW * N_COL
    flat_tiles = tile_values.reshape(ndevices * TILES, TILE, TILE)
    flat_rows = tile_row.reshape(-1).astype(jnp.int32)
    flat_cols = tile_col.reshape(-1).astype(jnp.int32)
    owner = jnp.repeat(jnp.arange(ndevices, dtype=jnp.int32), TILES)
    slot_ids = jnp.tile(jnp.arange(TILES, dtype=jnp.int32), ndevices)
    live = (slot_ids < tile_count.reshape(-1)[owner]).astype(jnp.float32)
    page_start = (owner // N_COL * P_BLK + flat_rows * TILE).astype(jnp.int32)
    feat_start = (owner % N_COL * F_BLK + flat_cols * TILE).astype(jnp.int32)

    def accumulate(source, transposed, src_starts, dst_starts, rows_out):
        if transposed:
            dims = (((0,), (0,)), ((), ()))
        else:
            dims = (((1,), (0,)), ((), ()))

        def step(total, item):
            tile, src, dst, weight = item
            block = lax.dynamic_slice_in_dim(source, src, TILE, 0)
            term = lax.dot_general(tile, block, dims, preferred_element_type=jnp.float32) * weight
            old = lax.dynamic_slice_in_dim(total, dst, TILE, 0)
            return (lax.dynamic_update_slice_in_dim(total, old + term, dst, 0), None)
        start = jnp.zeros((rows_out, C), jnp.float32)
        total, _ = lax.scan(step, start, (flat_tiles, src_starts, dst_starts, live))
        return total
    feature_sums = accumulate(page_scores, True, page_start, feat_start, FEATS)
    feature_scores = clamp_scores(feature_sums, feature_degree, feature_seed, feature_label).astype(jnp.bfloat16)
    page_sums = accumulate(feature_scores, False, feat_start, page_start, PAGES)
    return clamp_scores(page_sums, page_degree, page_seed, page_label).astype(jnp.bfloat16)
```

```python
import functools

import jax
import jax.numpy as jnp
from jax import lax
from jax.experimental import pallas as pl
from jax.experimental.pallas import tpu as pltpu
from jax.sharding import Mesh, PartitionSpec as P

BF16 = jnp.bfloat16
F32 = jnp.float32
ROW = ("zlo", "y", "core")
COL = ("zhi", "x")
TILE_DOT = (((1,), (0,)), ((), ()))
TILE_T_DOT = (((0,), (0,)), ((), ()))


def clamp(sums, degree, known, label):
    classes = lax.broadcasted_iota(jnp.int32, sums.shape, 1)
    hot = (label[:, None] == classes).astype(F32)
    scaled = sums * lax.rsqrt(degree.astype(F32))[:, None]
    return jnp.where(known[:, None] == 1, hot, scaled).astype(BF16)


def add(*terms):
    total = terms[0].astype(F32)
    for term in terms[1:]:
        total = total + term.astype(F32)
    return total


def feature_kernel(row_ref, col_ref, count_ref, tiles, pages, out, tile_buf, page_buf, acc, sems):
    edge = tile_buf.shape[1]
    count = count_ref[0]

    def copies(slot):
        src = pl.multiple_of(row_ref[slot] * edge, edge)
        return (
            pltpu.make_async_copy(tiles.at[slot], tile_buf.at[slot], sems.at[0, slot]),
            pltpu.make_async_copy(pages.at[pl.ds(src, edge)], page_buf.at[slot], sems.at[1, slot]),
        )

    @pl.loop(0, count)
    def _(slot):
        for copy in copies(slot):
            copy.start()

    acc[...] = jnp.zeros_like(acc)

    @pl.loop(0, count)
    def _(slot):
        for copy in copies(slot):
            copy.wait()
        dst = pl.ds(pl.multiple_of(col_ref[slot] * edge, edge), edge)
        acc[dst, :] += lax.dot_general(
            tile_buf[slot], page_buf[slot], TILE_T_DOT, preferred_element_type=F32
        )

    out[...] = acc[...].astype(BF16)


def feature_partials(rows, cols, count, tiles, pages, feats):
    slots, edge, _ = tiles.shape
    classes = pages.shape[1]
    return pl.pallas_call(
        feature_kernel,
        out_shape=jax.ShapeDtypeStruct((feats, classes), BF16),
        in_specs=[pl.BlockSpec(memory_space=pltpu.SMEM)] * 3
        + [pl.BlockSpec(memory_space=pl.ANY)] * 2,
        out_specs=pl.BlockSpec(memory_space=pltpu.VMEM),
        scratch_shapes=[
            pltpu.VMEM((slots, edge, edge), BF16),
            pltpu.VMEM((slots, edge, classes), BF16),
            pltpu.VMEM((feats, classes), F32),
            pltpu.SemaphoreType.DMA((2, slots)),
        ],
        compiler_params=pltpu.CompilerParams(vmem_limit_bytes=32 << 20),
        cost_estimate=pl.CostEstimate(
            flops=2 * slots * edge * edge * classes,
            bytes_accessed=2 * slots * edge * (edge + classes),
            transcendentals=0,
        ),
        name="feature_partials",
    )(rows, cols, count, tiles, pages)


def page_kernel(deltas, per, row_ref, col_ref, count_ref, place, tiles, feats, *rest):
    n_out = 2 * len(deltas)
    outs, (tile_buf, acc, head, nxt, sems) = rest[:n_out], rest[n_out:]
    edge = tile_buf.shape[1]
    half = edge // 2
    page_tiles = head.shape[0]
    count = count_ref[0]

    @pl.loop(0, page_tiles)
    def _(r):
        head[r] = -1

    @pl.loop(0, count)
    def _(slot):
        r = row_ref[slot]
        nxt[slot] = head[r]
        head[r] = slot

    def copy(slot):
        return pltpu.make_async_copy(tiles.at[slot], tile_buf.at[slot], sems.at[slot])

    def page_tile(delta, index):
        ahead = index // per
        owner = lax.rem(place[1] + ahead, 4) * 4 + lax.rem(place[0] + delta, 4)
        return owner * per + lax.rem(index, per)

    for delta in deltas:

        @pl.loop(0, 4 * per)
        def _(index):
            def body(slot):
                copy(slot).start()
                return nxt[slot]

            lax.while_loop(lambda s: s >= 0, body, head[page_tile(delta, index)])

    for i, delta in enumerate(deltas):

        @pl.loop(0, 4 * per)
        def _(index):
            first = head[page_tile(delta, index)]

            @pl.when(first < 0)
            def _():
                outs[2 * i][index] = jnp.zeros((half, acc.shape[1]), BF16)
                outs[2 * i + 1][index] = jnp.zeros((half, acc.shape[1]), BF16)

            @pl.when(first >= 0)
            def _():
                def product(slot):
                    copy(slot).wait()
                    src = pl.ds(pl.multiple_of(col_ref[slot] * edge, edge), edge)
                    return lax.dot_general(
                        tile_buf[slot], feats[src, :], TILE_DOT, preferred_element_type=F32
                    )

                acc[...] = product(first)

                def body(slot):
                    acc[...] += product(slot)
                    return nxt[slot]

                lax.while_loop(lambda s: s >= 0, body, nxt[first])
                outs[2 * i][index] = acc[:half, :].astype(BF16)
                outs[2 * i + 1][index] = acc[half:, :].astype(BF16)


def page_partials(deltas, rows, cols, count, place, tiles, feats, page_tiles):
    slots, edge, _ = tiles.shape
    classes = feats.shape[1]
    per = page_tiles // 16
    piece = jax.ShapeDtypeStruct((4 * per, edge // 2, classes), BF16)
    out = pl.pallas_call(
        functools.partial(page_kernel, deltas, per),
        out_shape=[piece] * (2 * len(deltas)),
        in_specs=[pl.BlockSpec(memory_space=pltpu.SMEM)] * 4
        + [pl.BlockSpec(memory_space=pl.ANY), pl.BlockSpec(memory_space=pltpu.VMEM)],
        out_specs=[pl.BlockSpec(memory_space=pltpu.VMEM)] * (2 * len(deltas)),
        scratch_shapes=[
            pltpu.VMEM((slots, edge, edge), BF16),
            pltpu.VMEM((edge, classes), F32),
            pltpu.SMEM((page_tiles,), jnp.int32),
            pltpu.SMEM((slots,), jnp.int32),
            pltpu.SemaphoreType.DMA((slots,)),
        ],
        compiler_params=pltpu.CompilerParams(vmem_limit_bytes=32 << 20),
        cost_estimate=pl.CostEstimate(
            flops=2 * slots * edge * edge * classes * len(deltas) // 4,
            bytes_accessed=2 * slots * edge * edge * len(deltas) // 4,
            transcendentals=0,
        ),
        name="page_partials",
    )(rows, cols, count, place, tiles, feats)
    return [out[2 * i : 2 * i + 2] for i in range(len(deltas))]


def shift(x, axis, by):
    return lax.ppermute(x, axis, [(i, (i + by) % 4) for i in range(4)])


def ring_sums(pieces, axis):
    far_up = shift(pieces[2][0], axis, 1)
    far_down = shift(pieces[2][1], axis, 3)
    near_up = shift(pieces[1][1], axis, 1)
    near_down = shift(pieces[3][0], axis, 3)
    up = shift(add(far_up, pieces[1][0]).astype(BF16), axis, 1)
    down = shift(add(far_down, pieces[3][1]).astype(BF16), axis, 3)
    return add(pieces[0][0], near_down, up), add(pieces[0][1], near_up, down)


def local(
    page_scores,
    tile_values,
    tile_row,
    tile_col,
    tile_count,
    page_seed,
    page_label,
    page_degree,
    feature_seed,
    feature_label,
    feature_degree,
):
    tiles = tile_values[0, 0]
    rows, cols = tile_row[0, 0], tile_col[0, 0]
    count = tile_count[0]
    edge = tiles.shape[-1]
    feats, classes = feature_seed.shape[0], page_scores.shape[1]
    page_tiles = page_scores.shape[0] // edge
    share = feats // 16

    partial = feature_partials(rows, cols, count, tiles, page_scores, feats)
    parts = lax.all_to_all(partial.reshape(16, share, classes), ROW, 0, 0)
    mine = lax.axis_index(ROW) * share

    def own(x):
        return lax.dynamic_slice_in_dim(x, mine, share, 0)

    scores = clamp(
        parts.astype(F32).sum(0), own(feature_degree), own(feature_seed), own(feature_label)
    )
    feature_scores = lax.all_to_all(
        jnp.broadcast_to(scores[None], (16, share, classes)), ROW, 0, 0
    ).reshape(feats, classes)

    place = jnp.stack([lax.axis_index("x"), lax.axis_index("zhi")]).astype(jnp.int32)
    pieces = {}
    (pieces[2],) = page_partials(
        (2,), rows, cols, count, place, tiles, feature_scores, page_tiles
    )
    pieces[1], pieces[3], pieces[0] = page_partials(
        (1, 3, 0), rows, cols, count, place, tiles, feature_scores, page_tiles
    )
    first = ring_sums(pieces, "x")
    per = page_tiles // 16
    halves = [h.astype(BF16).reshape(4, per, edge // 2, classes) for h in first]
    top, bottom = ring_sums([[h[d] for h in halves] for d in range(4)], "zhi")
    sums = jnp.stack([top, bottom], 1).reshape(per * edge, classes)
    return clamp(sums, page_degree, page_seed, page_label)


def solution(mesh):
    parts = Mesh(mesh.devices.reshape(2, 4, 2, 4, 4), ROW + COL)
    in_specs = (
        P(ROW, None),
        P(ROW, COL, None, None, None),
        P(ROW, COL, None),
        P(ROW, COL, None),
        P(ROW, COL),
        P(ROW + COL),
        P(ROW + COL),
        P(ROW + COL),
        P(COL),
        P(COL),
        P(COL),
    )
    return jax.shard_map(
        local, mesh=parts, in_specs=in_specs, out_specs=P(ROW + COL, None), check_vma=False
    )
```

```python
import functools

import jax
import jax.numpy as jnp
from jax import lax
from jax.experimental import pallas as pl
from jax.experimental.pallas import tpu as pltpu
from jax.sharding import Mesh, PartitionSpec as P

BF16 = jnp.bfloat16
F32 = jnp.float32
ROW = ("zlo", "y", "core")
CHIPS = ("zlo", "y")
COL = ("zhi", "x")
TILE_DOT = (((1,), (0,)), ((), ()))
TILE_T_DOT = (((0,), (0,)), ((), ()))
SMEM = pl.BlockSpec(memory_space=pltpu.SMEM)
HBM = pl.BlockSpec(memory_space=pl.ANY)
VMEM = pl.BlockSpec(memory_space=pltpu.VMEM)


def clamp(sums, degree, known, label):
    classes = lax.broadcasted_iota(jnp.int32, sums.shape, 1)
    hot = (label[:, None] == classes).astype(F32)
    scaled = sums * lax.rsqrt(degree.astype(F32))[:, None]
    return jnp.where(known[:, None] == 1, hot, scaled).astype(BF16)


def add(*terms):
    total = terms[0].astype(F32)
    for term in terms[1:]:
        total = total + term.astype(F32)
    return total


def feature_kernel(
    row_ref, col_ref, count_ref, place, tiles, pages, own, other, tile_buf, page_buf, acc, sems
):
    edge = tile_buf.shape[1]
    half = edge // 2
    count = count_ref[0]
    core = place[2]

    def copies(slot):
        src = pl.multiple_of(row_ref[slot] * edge, edge)
        return (
            pltpu.make_async_copy(tiles.at[slot], tile_buf.at[slot], sems.at[0, slot]),
            pltpu.make_async_copy(pages.at[pl.ds(src, edge)], page_buf.at[slot], sems.at[1, slot]),
        )

    @pl.loop(0, count)
    def _(slot):
        for copy in copies(slot):
            copy.start()

    acc[...] = jnp.zeros_like(acc)

    @pl.loop(0, count)
    def _(slot):
        for copy in copies(slot):
            copy.wait()
        acc[col_ref[slot]] += lax.dot_general(
            page_buf[slot], tile_buf[slot], TILE_T_DOT, preferred_element_type=F32
        )

    for low, high, here in ((own, other, 0), (other, own, 1)):

        @pl.when(core == here)
        def _():
            @pl.loop(0, acc.shape[0])
            def _(tile):
                low[tile] = acc[tile, :, :half].T
                high[tile] = acc[tile, :, half:].T


def feature_partials(rows, cols, count, place, tiles, pages, feats):
    slots, edge, _ = tiles.shape
    classes = pages.shape[1]
    halves = jax.ShapeDtypeStruct((feats // edge, edge // 2, classes), F32)
    return pl.pallas_call(
        feature_kernel,
        out_shape=[halves, halves],
        in_specs=[SMEM] * 4 + [HBM] * 2,
        out_specs=[VMEM] * 2,
        scratch_shapes=[
            pltpu.VMEM((slots, edge, edge), BF16),
            pltpu.VMEM((slots, edge, classes), BF16),
            pltpu.VMEM((feats // edge, classes, edge), F32),
            pltpu.SemaphoreType.DMA((2, slots)),
        ],
        compiler_params=pltpu.CompilerParams(vmem_limit_bytes=56 << 20),
        cost_estimate=pl.CostEstimate(
            flops=2 * slots * edge * edge * classes,
            bytes_accessed=2 * slots * edge * (edge + classes),
            transcendentals=0,
        ),
        name="feature_partials",
    )(rows, cols, count, place, tiles, pages)


def page_kernel(deltas, straight, per, row_ref, col_ref, count_ref, place, tiles, mine, partner, *rest):
    n_out = 2 * len(deltas)
    outs, rest = rest[:n_out], rest[n_out:]
    if straight:
        first_out, rest = rest[0], rest[1:]
    tile_buf, feats, acc, head, nxt, sems, feat_sems = rest
    edge = tile_buf.shape[1]
    half = edge // 2
    span = 4 * per
    page_tiles = head.shape[0]
    count = count_ref[0]
    core = place[2]

    for which, source in ((core, mine), (1 - core, partner)):
        pltpu.make_async_copy(source, feats.at[which], feat_sems.at[which]).start()

    @pl.loop(0, page_tiles, unroll=8)
    def _(r):
        head[r] = -1

    def copy(slot):
        return pltpu.make_async_copy(tiles.at[slot], tile_buf.at[slot], sems.at[slot])

    @pl.loop(0, count)
    def _(slot):
        r = row_ref[slot]
        owner, k = r // per, lax.rem(r, per)
        ahead = lax.rem(lax.rem(owner, 4) - place[0] + 4, 4)
        r = ahead * span + lax.rem(owner // 4 - place[1] + 4, 4) * per + k
        wanted = functools.reduce(jnp.logical_or, [ahead == d for d in deltas])
        if straight:
            wanted = jnp.logical_or(wanted, k == 0)

        @pl.when(wanted)
        def _():
            copy(slot).start()
            nxt[slot] = head[r]
            head[r] = slot

    for out in outs:
        out[...] = jnp.zeros_like(out)
    if straight:
        first_out[...] = jnp.zeros_like(first_out)

    for which, source in ((core, mine), (1 - core, partner)):
        pltpu.make_async_copy(source, feats.at[which], feat_sems.at[which]).wait()

    def product(slot):
        copy(slot).wait()
        col = col_ref[slot]
        return lax.dot_general(
            tile_buf[slot, :, :half], feats[0, col], TILE_DOT, preferred_element_type=F32
        ) + lax.dot_general(
            tile_buf[slot, :, half:], feats[1, col], TILE_DOT, preferred_element_type=F32
        )

    def visit(delta, index, j):
        first = head[delta * span + index]
        second, k = index // per, lax.rem(index, per)

        @pl.when(first >= 0)
        def _():
            acc[...] = product(first)

            def body(slot):
                acc[...] += product(slot)
                return nxt[slot]

            lax.while_loop(lambda s: s >= 0, body, nxt[first])
            if straight:

                @pl.when(k == 0)
                def _():
                    slow = lax.rem(place[1] + second, 4)
                    fast = lax.rem(place[0] + delta, 4)
                    first_out[slow, fast] = acc[:half, :].astype(BF16)

            for i in range(len(deltas)):

                @pl.when(jnp.logical_and(j == i, k == 0))
                def _():
                    outs[2 * i][second, 0] = acc[half:, :].astype(BF16)

                @pl.when(jnp.logical_and(j == i, k > 0))
                def _():
                    outs[2 * i][second, k] = acc[:half, :].astype(BF16)
                    outs[2 * i + 1][second, k - 1] = acc[half:, :].astype(BF16)

    others = [d for d in range(4) if d not in deltas] if straight else []
    walk = [(d, j, 1) for j, d in enumerate(deltas)] + [(d, -1, per) for d in others]

    @pl.loop(0, len(walk))
    def _(w):
        delta, j, step = [
            functools.reduce(
                lambda v, n: jnp.where(w == n, walk[n][f], v), range(1, len(walk)), jnp.int32(walk[0][f])
            )
            for f in range(3)
        ]

        @pl.loop(0, span // step)
        def _(i):
            visit(delta, i * step, j)


def page_partials(deltas, straight, rows, cols, count, place, tiles, mine, partner, page_tiles):
    slots, edge, _ = tiles.shape
    classes = mine.shape[-1]
    per = page_tiles // 16
    half = edge // 2
    shapes = [(4, per, half, classes), (4, per - 1, half, classes)] * len(deltas)
    if straight:
        shapes.append((4, 4, half, classes))
    share = len(deltas) + (1 if straight else 0)
    out = pl.pallas_call(
        functools.partial(page_kernel, deltas, straight, per),
        out_shape=[jax.ShapeDtypeStruct(s, BF16) for s in shapes],
        in_specs=[SMEM] * 4 + [HBM] * 3,
        out_specs=[VMEM] * len(shapes),
        scratch_shapes=[
            pltpu.VMEM((slots, edge, edge), BF16),
            pltpu.VMEM((2,) + mine.shape, BF16),
            pltpu.VMEM((edge, classes), F32),
            pltpu.SMEM((page_tiles,), jnp.int32),
            pltpu.SMEM((slots,), jnp.int32),
            pltpu.SemaphoreType.DMA((slots,)),
            pltpu.SemaphoreType.DMA((2,)),
        ],
        compiler_params=pltpu.CompilerParams(vmem_limit_bytes=54 << 20),
        cost_estimate=pl.CostEstimate(
            flops=2 * slots * edge * edge * classes * share // 4,
            bytes_accessed=2 * slots * edge * edge * share // 4,
            transcendentals=0,
        ),
        name="page_partials",
    )(rows, cols, count, place, tiles, mine, partner)
    return [out[2 * i : 2 * i + 2] for i in range(len(deltas))], out[-1]


def shift(x, axis, by):
    return lax.ppermute(x, axis, [(i, (i + by) % 4) for i in range(4)])


def ring_terms(pieces, axis):
    far_up = shift(pieces[2][0], axis, 1)
    far_down = shift(pieces[2][1], axis, 3)
    near_up = shift(pieces[1][1], axis, 1)
    near_down = shift(pieces[3][0], axis, 3)
    up = shift(add(far_up, pieces[1][0]).astype(BF16), axis, 1)
    down = shift(add(far_down, pieces[3][1]).astype(BF16), axis, 3)
    return (pieces[0][0], near_down, up), (pieces[0][1], near_up, down)


def final_kernel(scale, base, straight, a0, a1, a2, b0, b1, b2, out):
    half = straight.shape[1]
    per = a0.shape[0]

    def put(unit, sums):
        rows = pl.ds(unit * half, half)
        out[rows, :] = (sums * scale[rows, :] + base[rows, :]).astype(BF16)

    put(0, add(*[straight[i] for i in range(4)]))
    for k in range(per):
        put(1 if k == 0 else 2 * k, add(a0[k], a1[k], a2[k]))
        if k:
            put(2 * k + 1, add(b0[k - 1], b1[k - 1], b2[k - 1]))


def local(
    page_scores,
    tile_values,
    tile_row,
    tile_col,
    tile_count,
    page_seed,
    page_label,
    page_degree,
    feature_seed,
    feature_label,
    feature_degree,
):
    tiles = tile_values[0, 0]
    rows, cols = tile_row[0, 0], tile_col[0, 0]
    count = tile_count[0]
    edge = tiles.shape[-1]
    half = edge // 2
    feats, classes = feature_seed.shape[0], page_scores.shape[1]
    page_tiles = page_scores.shape[0] // edge
    per = page_tiles // 16
    place = jnp.stack([lax.axis_index(a) for a in ("x", "zhi", "core")]).astype(jnp.int32)

    def swap(x):
        return lax.ppermute(x, "core", [(0, 1), (1, 0)])

    kept, other = feature_partials(rows, cols, count, place, tiles, page_scores, feats)
    pair = add(kept, swap(other)).astype(BF16)
    parts = lax.all_to_all(pair, CHIPS, 0, 0)
    first = lax.axis_index(ROW) * half

    def own(x):
        return lax.dynamic_slice_in_dim(x, first, half, 0)

    scores = clamp(
        parts.astype(F32).sum(0), own(feature_degree), own(feature_seed), own(feature_label)
    )
    mine = lax.all_to_all(jnp.broadcast_to(scores[None], pair.shape), CHIPS, 0, 0)
    partner = swap(mine)

    known = (page_seed == 1)[:, None]
    hot = page_label[:, None] == lax.broadcasted_iota(jnp.int32, (per * edge, classes), 1)
    base = jnp.where(jnp.logical_and(known, hot), 1.0, 0.0).astype(F32)
    scale = jnp.where(known, 0.0, lax.rsqrt(page_degree.astype(F32))[:, None])
    scale = jnp.broadcast_to(scale, base.shape)

    common = (rows, cols, count, place, tiles, mine, partner, page_tiles)
    pieces = {}
    (pieces[2],), _ = page_partials((2,), False, *common)
    (pieces[1], pieces[3]), _ = page_partials((1, 3), False, *common)
    (pieces[0],), straight = page_partials((0,), True, *common)
    base, scale, pieces[0] = lax.optimization_barrier((base, scale, pieces[0]))

    halves = [add(*t).astype(BF16) for t in ring_terms(pieces, "x")]
    straight = lax.all_to_all(straight, "zhi", 0, 0)
    straight = lax.all_to_all(straight.astype(F32).sum(0).astype(BF16), "x", 0, 0)
    even, odd = ring_terms([[h[d] for h in halves] for d in range(4)], "zhi")

    return pl.pallas_call(
        final_kernel,
        out_shape=jax.ShapeDtypeStruct(base.shape, BF16),
        in_specs=[VMEM] * 9,
        out_specs=VMEM,
        name="final_sums",
    )(scale, base, straight, *even, *odd)


def solution(mesh):
    parts = Mesh(mesh.devices.reshape(2, 4, 2, 4, 4), ROW + COL)
    in_specs = (
        P(ROW, None),
        P(ROW, COL, None, None, None),
        P(ROW, COL, None),
        P(ROW, COL, None),
        P(ROW, COL),
        P(ROW + COL),
        P(ROW + COL),
        P(ROW + COL),
        P(COL),
        P(COL),
        P(COL),
    )
    return jax.shard_map(
        local, mesh=parts, in_specs=in_specs, out_specs=P(ROW + COL, None), check_vma=False
    )
```

```python
import functools

import jax
import jax.numpy as jnp
from jax import lax
from jax.experimental import pallas as pl
from jax.experimental.pallas import tpu as pltpu
from jax.sharding import Mesh, PartitionSpec as P

BF16 = jnp.bfloat16
F32 = jnp.float32
ROW = ("zlo", "y", "core")
CHIPS = ("zlo", "y")
COL = ("zhi", "x")
TILE_DOT = (((1,), (0,)), ((), ()))
TILE_T_DOT = (((0,), (0,)), ((), ()))
SMEM = pl.BlockSpec(memory_space=pltpu.SMEM)
HBM = pl.BlockSpec(memory_space=pl.ANY)
VMEM = pl.BlockSpec(memory_space=pltpu.VMEM)


def clamp(sums, degree, known, label):
    classes = lax.broadcasted_iota(jnp.int32, sums.shape, 1)
    hot = (label[:, None] == classes).astype(F32)
    scaled = sums * lax.rsqrt(degree.astype(F32))[:, None]
    return jnp.where(known[:, None] == 1, hot, scaled).astype(BF16)


def add(*terms):
    total = terms[0].astype(F32)
    for term in terms[1:]:
        total = total + term.astype(F32)
    return total


def feature_kernel(
    row_ref, col_ref, count_ref, place, tiles, pages, own, other, tile_buf, page_buf, acc, sems
):
    edge = tile_buf.shape[1]
    half = edge // 2
    count = count_ref[0]
    core = place[2]

    def copies(slot):
        src = pl.multiple_of(row_ref[slot] * edge, edge)
        return (
            pltpu.make_async_copy(tiles.at[slot], tile_buf.at[slot], sems.at[0, slot]),
            pltpu.make_async_copy(pages.at[pl.ds(src, edge)], page_buf.at[slot], sems.at[1, slot]),
        )

    @pl.loop(0, count)
    def _(slot):
        for copy in copies(slot):
            copy.start()

    acc[...] = jnp.zeros_like(acc)

    @pl.loop(0, count)
    def _(slot):
        for copy in copies(slot):
            copy.wait()
        acc[col_ref[slot]] += lax.dot_general(
            page_buf[slot], tile_buf[slot], TILE_T_DOT, preferred_element_type=F32
        )

    for low, high, here in ((own, other, 0), (other, own, 1)):

        @pl.when(core == here)
        def _():
            @pl.loop(0, acc.shape[0])
            def _(tile):
                low[tile] = acc[tile, :, :half].T
                high[tile] = acc[tile, :, half:].T


def feature_partials(rows, cols, count, place, tiles, pages, feats):
    slots, edge, _ = tiles.shape
    classes = pages.shape[1]
    halves = jax.ShapeDtypeStruct((feats // edge, edge // 2, classes), F32)
    return pl.pallas_call(
        feature_kernel,
        out_shape=[halves, halves],
        in_specs=[SMEM] * 4 + [HBM] * 2,
        out_specs=[VMEM] * 2,
        scratch_shapes=[
            pltpu.VMEM((slots, edge, edge), BF16),
            pltpu.VMEM((slots, edge, classes), BF16),
            pltpu.VMEM((feats // edge, classes, edge), F32),
            pltpu.SemaphoreType.DMA((2, slots)),
        ],
        compiler_params=pltpu.CompilerParams(vmem_limit_bytes=50 << 20),
        cost_estimate=pl.CostEstimate(
            flops=2 * slots * edge * edge * classes,
            bytes_accessed=2 * slots * edge * (edge + classes),
            transcendentals=0,
        ),
        name="feature_partials",
    )(rows, cols, count, place, tiles, pages)


def page_kernel(deltas, straight, per, row_ref, col_ref, count_ref, place, tiles, mine, partner, *rest):
    n_out = 2 * len(deltas)
    outs, rest = rest[:n_out], rest[n_out:]
    if straight:
        first_out, rest = rest[0], rest[1:]
    tile_buf, feats, acc, head, nxt, sems, feat_sems = rest
    edge = tile_buf.shape[1]
    half = edge // 2
    span = 4 * per
    page_tiles = head.shape[0]
    count = count_ref[0]
    core = place[2]

    def feature_copies():
        for which, source in ((core, mine), (1 - core, partner)):
            part = pl.ds(pl.multiple_of(which * half, half), half)
            yield pltpu.make_async_copy(source, feats.at[:, part], feat_sems.at[which])

    for copy in feature_copies():
        copy.start()

    @pl.loop(0, page_tiles, unroll=8)
    def _(r):
        head[r] = -1

    def tile_copy(slot):
        return pltpu.make_async_copy(tiles.at[slot], tile_buf.at[slot], sems.at[slot])

    @pl.loop(0, count)
    def _(slot):
        r = row_ref[slot]
        owner, k = r // per, lax.rem(r, per)
        ahead = lax.rem(lax.rem(owner, 4) - place[0] + 4, 4)
        r = ahead * span + lax.rem(owner // 4 - place[1] + 4, 4) * per + k
        wanted = functools.reduce(jnp.logical_or, [ahead == d for d in deltas])
        if straight:
            wanted = jnp.logical_or(wanted, k == 0)

        @pl.when(wanted)
        def _():
            tile_copy(slot).start()
            nxt[slot] = head[r]
            head[r] = slot

    for out in outs:
        out[...] = jnp.zeros_like(out)
    if straight:
        first_out[...] = jnp.zeros_like(first_out)

    for copy in feature_copies():
        copy.wait()

    def product(slot):
        tile_copy(slot).wait()
        return lax.dot_general(
            tile_buf[slot], feats[col_ref[slot]], TILE_DOT, preferred_element_type=F32
        )

    def visit(delta, index, j):
        first = head[delta * span + index]
        second, k = index // per, lax.rem(index, per)

        @pl.when(first >= 0)
        def _():
            acc[...] = product(first)

            def body(slot):
                acc[...] += product(slot)
                return nxt[slot]

            lax.while_loop(lambda s: s >= 0, body, nxt[first])
            if straight:

                @pl.when(k == 0)
                def _():
                    slow = lax.rem(place[1] + second, 4)
                    fast = lax.rem(place[0] + delta, 4)
                    first_out[slow, fast] = acc[:half, :].astype(BF16)

            for i in range(len(deltas)):

                @pl.when(jnp.logical_and(j == i, k == 0))
                def _():
                    outs[2 * i][second, 0] = acc[half:, :].astype(BF16)

                @pl.when(jnp.logical_and(j == i, k > 0))
                def _():
                    outs[2 * i][second, k] = acc[:half, :].astype(BF16)
                    outs[2 * i + 1][second, k - 1] = acc[half:, :].astype(BF16)

    others = [d for d in range(4) if d not in deltas] if straight else []
    walk = [(d, j, 1) for j, d in enumerate(deltas)] + [(d, -1, per) for d in others]

    @pl.loop(0, len(walk))
    def _(w):
        delta, j, step = [
            functools.reduce(
                lambda v, n: jnp.where(w == n, walk[n][f], v), range(1, len(walk)), jnp.int32(walk[0][f])
            )
            for f in range(3)
        ]

        @pl.loop(0, span // step)
        def _(i):
            visit(delta, i * step, j)


def page_partials(deltas, straight, rows, cols, count, place, tiles, mine, partner, page_tiles):
    slots, edge, _ = tiles.shape
    classes = mine.shape[-1]
    per = page_tiles // 16
    half = edge // 2
    shapes = [(4, per, half, classes), (4, per - 1, half, classes)] * len(deltas)
    if straight:
        shapes.append((4, 4, half, classes))
    share = len(deltas) + (1 if straight else 0)
    out = pl.pallas_call(
        functools.partial(page_kernel, deltas, straight, per),
        out_shape=[jax.ShapeDtypeStruct(s, BF16) for s in shapes],
        in_specs=[SMEM] * 4 + [HBM] * 3,
        out_specs=[VMEM] * len(shapes),
        scratch_shapes=[
            pltpu.VMEM((slots, edge, edge), BF16),
            pltpu.VMEM((mine.shape[0], edge, classes), BF16),
            pltpu.VMEM((edge, classes), F32),
            pltpu.SMEM((page_tiles,), jnp.int32),
            pltpu.SMEM((slots,), jnp.int32),
            pltpu.SemaphoreType.DMA((slots,)),
            pltpu.SemaphoreType.DMA((2,)),
        ],
        compiler_params=pltpu.CompilerParams(vmem_limit_bytes=50 << 20),
        cost_estimate=pl.CostEstimate(
            flops=2 * slots * edge * edge * classes * share // 4,
            bytes_accessed=2 * slots * edge * edge * share // 4,
            transcendentals=0,
        ),
        name="page_partials",
    )(rows, cols, count, place, tiles, mine, partner)
    return [out[2 * i : 2 * i + 2] for i in range(len(deltas))], out[-1]


def shift(x, axis, by):
    return lax.ppermute(x, axis, [(i, (i + by) % 4) for i in range(4)])


def ring_terms(pieces, axis):
    far_up = shift(pieces[2][0], axis, 1)
    far_down = shift(pieces[2][1], axis, 3)
    near_up = shift(pieces[1][1], axis, 1)
    near_down = shift(pieces[3][0], axis, 3)
    up = shift(add(far_up, pieces[1][0]).astype(BF16), axis, 1)
    down = shift(add(far_down, pieces[3][1]).astype(BF16), axis, 3)
    return (pieces[0][0], near_down, up), (pieces[0][1], near_up, down)


def final_kernel(scale, base, straight, a0, a1, a2, b0, b1, b2, out):
    half = straight.shape[1]
    per = a0.shape[0]

    def put(unit, sums):
        rows = pl.ds(unit * half, half)
        out[rows, :] = (sums * scale[rows, :] + base[rows, :].astype(F32)).astype(BF16)

    put(0, add(*[straight[i] for i in range(4)]))
    for k in range(per):
        put(1 if k == 0 else 2 * k, add(a0[k], a1[k], a2[k]))
        if k:
            put(2 * k + 1, add(b0[k - 1], b1[k - 1], b2[k - 1]))


def local(
    page_scores,
    tile_values,
    tile_row,
    tile_col,
    tile_count,
    page_seed,
    page_label,
    page_degree,
    feature_seed,
    feature_label,
    feature_degree,
):
    tiles = tile_values[0, 0]
    rows, cols = tile_row[0, 0], tile_col[0, 0]
    count = tile_count[0]
    edge = tiles.shape[-1]
    half = edge // 2
    feats, classes = feature_seed.shape[0], page_scores.shape[1]
    page_tiles = page_scores.shape[0] // edge
    per = page_tiles // 16
    place = jnp.stack([lax.axis_index(a) for a in ("x", "zhi", "core")]).astype(jnp.int32)

    def swap(x):
        return lax.ppermute(x, "core", [(0, 1), (1, 0)])

    kept, other = feature_partials(rows, cols, count, place, tiles, page_scores, feats)
    pair = add(kept, swap(other)).astype(BF16)
    parts = lax.all_to_all(pair, CHIPS, 0, 0)
    first = lax.axis_index(ROW) * half

    def own(x):
        return lax.dynamic_slice_in_dim(x, first, half, 0)

    scores = clamp(
        parts.astype(F32).sum(0), own(feature_degree), own(feature_seed), own(feature_label)
    )
    mine = lax.all_to_all(jnp.broadcast_to(scores[None], pair.shape), CHIPS, 0, 0)
    partner = swap(mine)

    known = (page_seed == 1)[:, None]
    hot = page_label[:, None] == lax.broadcasted_iota(jnp.int32, (per * edge, classes), 1)
    base = jnp.where(jnp.logical_and(known, hot), 1.0, 0.0).astype(BF16)
    scale = jnp.where(known, 0.0, lax.rsqrt(page_degree.astype(F32))[:, None])
    scale = jnp.broadcast_to(scale, base.shape)

    def pages(deltas, straight, mine, partner):
        return page_partials(
            deltas, straight, rows, cols, count, place, tiles, mine, partner, page_tiles
        )

    (far,), _ = pages((2,), False, mine, partner)
    (ahead, behind), straight = pages((1, 3), True, mine, partner)
    straight = lax.all_to_all(straight, "zhi", 0, 0)
    far_up = shift(far[0], "x", 1)
    far_down = shift(far[1], "x", 3)
    near_up = shift(ahead[1], "x", 1)
    near_down = shift(behind[0], "x", 3)
    up = add(far_up, ahead[0]).astype(BF16)
    down = add(far_down, behind[1]).astype(BF16)
    up, down, mine, partner = lax.optimization_barrier((up, down, mine, partner))
    up = shift(up, "x", 1)
    down = shift(down, "x", 3)
    (here,), _ = pages((0,), False, mine, partner)
    base, scale, here = lax.optimization_barrier((base, scale, here))
    halves = [
        add(here[0], near_down, up).astype(BF16),
        add(here[1], near_up, down).astype(BF16),
    ]
    straight = lax.all_to_all(straight.astype(F32).sum(0).astype(BF16), "x", 0, 0)
    even, odd = ring_terms([[h[d] for h in halves] for d in range(4)], "zhi")

    return pl.pallas_call(
        final_kernel,
        out_shape=jax.ShapeDtypeStruct(base.shape, BF16),
        in_specs=[VMEM] * 9,
        out_specs=VMEM,
        name="final_sums",
    )(scale, base, straight, *even, *odd)


def solution(mesh):
    parts = Mesh(mesh.devices.reshape(2, 4, 2, 4, 4), ROW + COL)
    in_specs = (
        P(ROW, None),
        P(ROW, COL, None, None, None),
        P(ROW, COL, None),
        P(ROW, COL, None),
        P(ROW, COL),
        P(ROW + COL),
        P(ROW + COL),
        P(ROW + COL),
        P(COL),
        P(COL),
        P(COL),
    )
    return jax.shard_map(
        local, mesh=parts, in_specs=in_specs, out_specs=P(ROW + COL, None), check_vma=False
    )
```

```python
import functools

import jax
import jax.numpy as jnp
from jax import lax
from jax.experimental import pallas as pl
from jax.experimental.pallas import tpu as pltpu
from jax.sharding import Mesh, PartitionSpec as P

BF16 = jnp.bfloat16
F32 = jnp.float32
ROW = ("zlo", "y", "core")
CHIPS = ("zlo", "y")
COL = ("zhi", "x")
TILE_DOT = (((1,), (0,)), ((), ()))
TILE_T_DOT = (((0,), (0,)), ((), ()))
SMEM = pl.BlockSpec(memory_space=pltpu.SMEM)
HBM = pl.BlockSpec(memory_space=pl.ANY)
VMEM = pl.BlockSpec(memory_space=pltpu.VMEM)


def clamp(sums, degree, known, label):
    classes = lax.broadcasted_iota(jnp.int32, sums.shape, 1)
    hot = (label[:, None] == classes).astype(F32)
    scaled = sums * lax.rsqrt(degree.astype(F32))[:, None]
    return jnp.where(known[:, None] == 1, hot, scaled).astype(BF16)


def add(*terms):
    total = terms[0].astype(F32)
    for term in terms[1:]:
        total = total + term.astype(F32)
    return total


def feature_kernel(
    table, tiles, pages, own, other, tile_buf, page_buf, acc, sems
):
    slots, edge, _ = tile_buf.shape
    half = edge // 2
    count = table[2 * slots]
    core = table[2 * slots + 3]

    def copies(slot):
        src = pl.multiple_of(table[slot] * edge, edge)
        return (
            pltpu.make_async_copy(tiles.at[slot], tile_buf.at[slot], sems.at[0, slot]),
            pltpu.make_async_copy(pages.at[pl.ds(src, edge)], page_buf.at[slot], sems.at[1, slot]),
        )

    @pl.loop(0, count)
    def _(slot):
        for copy in copies(slot):
            copy.start()

    acc[...] = jnp.zeros_like(acc)

    @pl.loop(0, count)
    def _(slot):
        for copy in copies(slot):
            copy.wait()
        acc[table[slots + slot]] += lax.dot_general(
            page_buf[slot], tile_buf[slot], TILE_T_DOT, preferred_element_type=F32
        )

    for low, high, here in ((own, other, 0), (other, own, 1)):

        @pl.when(core == here)
        def _():
            @pl.loop(0, acc.shape[0])
            def _(tile):
                low[tile] = acc[tile, :, :half].T
                high[tile] = acc[tile, :, half:].T


def feature_partials(table, tiles, pages, feats):
    slots, edge, _ = tiles.shape
    classes = pages.shape[1]
    halves = jax.ShapeDtypeStruct((feats // edge, edge // 2, classes), F32)
    return pl.pallas_call(
        feature_kernel,
        out_shape=[halves, halves],
        in_specs=[SMEM] + [HBM] * 2,
        out_specs=[VMEM] * 2,
        scratch_shapes=[
            pltpu.VMEM((slots, edge, edge), BF16),
            pltpu.VMEM((slots, edge, classes), BF16),
            pltpu.VMEM((feats // edge, classes, edge), F32),
            pltpu.SemaphoreType.DMA((2, slots)),
        ],
        compiler_params=pltpu.CompilerParams(vmem_limit_bytes=50 << 20),
        cost_estimate=pl.CostEstimate(
            flops=2 * slots * edge * edge * classes,
            bytes_accessed=2 * slots * edge * (edge + classes),
            transcendentals=0,
        ),
        name="feature_partials",
    )(table, tiles, pages)


def page_kernel(deltas, straight, per, table, tiles, mine, partner, *rest):
    n_out = 2 * len(deltas)
    outs, rest = rest[:n_out], rest[n_out:]
    if straight:
        first_out, rest = rest[0], rest[1:]
    tile_buf, feats, acc, head, nxt, sems, feat_sems = rest
    slots, edge, _ = tile_buf.shape
    half = edge // 2
    span = 4 * per
    page_tiles = head.shape[0]
    count = table[2 * slots]
    core = table[2 * slots + 3]

    def feature_copies():
        for which, source in ((core, mine), (1 - core, partner)):
            part = pl.ds(pl.multiple_of(which * half, half), half)
            yield pltpu.make_async_copy(source, feats.at[:, part], feat_sems.at[which])

    for copy in feature_copies():
        copy.start()

    @pl.loop(0, page_tiles, unroll=8)
    def _(r):
        head[r] = -1

    def tile_copy(slot):
        return pltpu.make_async_copy(tiles.at[slot], tile_buf.at[slot], sems.at[slot])

    @pl.loop(0, count)
    def _(slot):
        r = table[slot]
        owner, k = r // per, lax.rem(r, per)
        ahead = lax.rem(lax.rem(owner, 4) - table[2 * slots + 1] + 4, 4)
        r = ahead * span + lax.rem(owner // 4 - table[2 * slots + 2] + 4, 4) * per + k
        wanted = functools.reduce(jnp.logical_or, [ahead == d for d in deltas])
        if straight:
            wanted = jnp.logical_or(wanted, k == 0)

        @pl.when(wanted)
        def _():
            tile_copy(slot).start()
            nxt[slot] = head[r]
            head[r] = slot

    for out in outs:
        out[...] = jnp.zeros_like(out)
    if straight:
        first_out[...] = jnp.zeros_like(first_out)

    for copy in feature_copies():
        copy.wait()

    def product(slot):
        tile_copy(slot).wait()
        return lax.dot_general(
            tile_buf[slot], feats[table[slots + slot]], TILE_DOT, preferred_element_type=F32
        )

    def visit(delta, index, j):
        first = head[delta * span + index]
        second, k = index // per, lax.rem(index, per)

        @pl.when(first >= 0)
        def _():
            acc[...] = product(first)

            def body(slot):
                acc[...] += product(slot)
                return nxt[slot]

            lax.while_loop(lambda s: s >= 0, body, nxt[first])
            if straight:

                @pl.when(k == 0)
                def _():
                    slow = lax.rem(table[2 * slots + 2] + second, 4)
                    first_out[slow, delta] = acc[:half, :].astype(BF16)

            for i in range(len(deltas)):

                @pl.when(jnp.logical_and(j == i, k == 0))
                def _():
                    outs[2 * i][second, 0] = acc[half:, :].astype(BF16)

                @pl.when(jnp.logical_and(j == i, k > 0))
                def _():
                    outs[2 * i][second, k] = acc[:half, :].astype(BF16)
                    outs[2 * i + 1][second, k - 1] = acc[half:, :].astype(BF16)

    others = [d for d in range(4) if d not in deltas] if straight else []
    walk = [(d, j, 1) for j, d in enumerate(deltas)] + [(d, -1, per) for d in others]

    @pl.loop(0, len(walk))
    def _(w):
        delta, j, step = [
            functools.reduce(
                lambda v, n: jnp.where(w == n, walk[n][f], v), range(1, len(walk)), jnp.int32(walk[0][f])
            )
            for f in range(3)
        ]

        @pl.loop(0, span // step)
        def _(i):
            visit(delta, i * step, j)


def page_partials(deltas, straight, table, tiles, mine, partner, page_tiles):
    slots, edge, _ = tiles.shape
    classes = mine.shape[-1]
    per = page_tiles // 16
    half = edge // 2
    shapes = [(4, per, half, classes), (4, per - 1, half, classes)] * len(deltas)
    if straight:
        shapes.append((4, 4, half, classes))
    share = len(deltas) + (1 if straight else 0)
    out = pl.pallas_call(
        functools.partial(page_kernel, deltas, straight, per),
        out_shape=[jax.ShapeDtypeStruct(s, BF16) for s in shapes],
        in_specs=[SMEM] + [HBM] * 3,
        out_specs=[VMEM] * len(shapes),
        scratch_shapes=[
            pltpu.VMEM((slots, edge, edge), BF16),
            pltpu.VMEM((mine.shape[0], edge, classes), BF16),
            pltpu.VMEM((edge, classes), F32),
            pltpu.SMEM((page_tiles,), jnp.int32),
            pltpu.SMEM((slots,), jnp.int32),
            pltpu.SemaphoreType.DMA((slots,)),
            pltpu.SemaphoreType.DMA((2,)),
        ],
        compiler_params=pltpu.CompilerParams(vmem_limit_bytes=50 << 20),
        cost_estimate=pl.CostEstimate(
            flops=2 * slots * edge * edge * classes * share // 4,
            bytes_accessed=2 * slots * edge * edge * share // 4,
            transcendentals=0,
        ),
        name="page_partials",
    )(table, tiles, mine, partner)
    return [out[2 * i : 2 * i + 2] for i in range(len(deltas))], out[-1]


def shift(x, axis, by):
    return lax.ppermute(x, axis, [(i, (i + by) % 4) for i in range(4)])


def ring_terms(pieces, axis):
    far_up = shift(pieces[2][0], axis, 1)
    far_down = shift(pieces[2][1], axis, 3)
    near_up = shift(pieces[1][1], axis, 1)
    near_down = shift(pieces[3][0], axis, 3)
    up = shift(add(far_up, pieces[1][0]).astype(BF16), axis, 1)
    down = shift(add(far_down, pieces[3][1]).astype(BF16), axis, 3)
    return (pieces[0][0], near_down, up), (pieces[0][1], near_up, down)


def final_kernel(scale, base, s0, s1, s2, s3, a0, a1, a2, b0, b1, b2, out):
    half = s0.shape[0]
    per = a0.shape[0]

    def put(unit, sums):
        rows = pl.ds(unit * half, half)
        out[rows, :] = (sums * scale[rows, :] + base[rows, :].astype(F32)).astype(BF16)

    put(0, add(s0[...], s1[...], s2[...], s3[...]))
    for k in range(per):
        put(1 if k == 0 else 2 * k, add(a0[k], a1[k], a2[k]))
        if k:
            put(2 * k + 1, add(b0[k - 1], b1[k - 1], b2[k - 1]))


def split_kernel(a, b, c, *outs):
    for d in range(4):
        outs[d][...] = add(a[d], b[d], c[d]).astype(BF16)


def split_sums(*terms):
    piece = jax.ShapeDtypeStruct(terms[0].shape[1:], BF16)
    return pl.pallas_call(
        split_kernel,
        out_shape=[piece] * 4,
        in_specs=[VMEM] * 3,
        out_specs=[VMEM] * 4,
        compiler_params=pltpu.CompilerParams(vmem_limit_bytes=16 << 20),
        cost_estimate=pl.CostEstimate(
            flops=2 * terms[0].size, bytes_accessed=8 * terms[0].size, transcendentals=0
        ),
        name="split_sums",
    )(*terms)


def local(
    page_scores,
    tile_values,
    tile_row,
    tile_col,
    tile_count,
    page_seed,
    page_label,
    page_degree,
    feature_seed,
    feature_label,
    feature_degree,
):
    tiles = tile_values[0, 0]
    edge = tiles.shape[-1]
    half = edge // 2
    feats, classes = feature_seed.shape[0], page_scores.shape[1]
    page_tiles = page_scores.shape[0] // edge
    per = page_tiles // 16
    place = jnp.stack([lax.axis_index(a) for a in ("x", "zhi", "core")]).astype(jnp.int32)
    table = jnp.concatenate([tile_row[0, 0], tile_col[0, 0], tile_count[0], place])

    def swap(x):
        return lax.ppermute(x, "core", [(0, 1), (1, 0)])

    kept, other = feature_partials(table, tiles, page_scores, feats)
    pair = add(kept, swap(other)).astype(BF16)
    parts = lax.all_to_all(pair, CHIPS, 0, 0)
    first = lax.axis_index(ROW) * half

    def own(x):
        return lax.dynamic_slice_in_dim(x, first, half, 0)

    scores = clamp(
        parts.astype(F32).sum(0), own(feature_degree), own(feature_seed), own(feature_label)
    )
    mine = lax.all_to_all(jnp.broadcast_to(scores[None], pair.shape), CHIPS, 0, 0)
    partner = swap(mine)

    known = (page_seed == 1)[:, None]
    hot = page_label[:, None] == lax.broadcasted_iota(jnp.int32, (per * edge, classes), 1)
    base = jnp.where(jnp.logical_and(known, hot), 1.0, 0.0).astype(BF16)
    scale = jnp.where(known, 0.0, lax.rsqrt(page_degree.astype(F32))[:, None])
    scale = jnp.broadcast_to(scale, base.shape)

    def pages(deltas, straight, mine, partner):
        return page_partials(
            deltas, straight, table, tiles, mine, partner, page_tiles
        )

    (far,), _ = pages((2,), False, mine, partner)
    (ahead, behind), straight = pages((1, 3), True, mine, partner)
    straight = lax.all_to_all(straight, "zhi", 0, 0)
    far_up = shift(far[0], "x", 1)
    far_down = shift(far[1], "x", 3)
    near_up = shift(ahead[1], "x", 1)
    near_down = shift(behind[0], "x", 3)
    up = add(far_up, ahead[0]).astype(BF16)
    down = add(far_down, behind[1]).astype(BF16)
    up, down, mine, partner = lax.optimization_barrier((up, down, mine, partner))
    up = shift(up, "x", 1)
    down = shift(down, "x", 3)
    (here,), _ = pages((0,), False, mine, partner)
    base, scale, here = lax.optimization_barrier((base, scale, here))
    halves = [split_sums(here[0], near_down, up), split_sums(here[1], near_up, down)]
    straight = add(*[straight[i] for i in range(4)]).astype(BF16)
    straight = [straight[0]] + [shift(straight[d], "x", d) for d in (1, 3, 2)]
    even, odd = ring_terms([[h[d] for h in halves] for d in range(4)], "zhi")

    return pl.pallas_call(
        final_kernel,
        out_shape=jax.ShapeDtypeStruct(base.shape, BF16),
        in_specs=[VMEM] * 12,
        out_specs=VMEM,
        compiler_params=pltpu.CompilerParams(vmem_limit_bytes=16 << 20),
        name="final_sums",
    )(scale, base, *straight, *even, *odd)


def solution(mesh):
    parts = Mesh(mesh.devices.reshape(2, 4, 2, 4, 4), ROW + COL)
    in_specs = (
        P(ROW, None),
        P(ROW, COL, None, None, None),
        P(ROW, COL, None),
        P(ROW, COL, None),
        P(ROW, COL),
        P(ROW + COL),
        P(ROW + COL),
        P(ROW + COL),
        P(COL),
        P(COL),
        P(COL),
    )
    return jax.shard_map(
        local, mesh=parts, in_specs=in_specs, out_specs=P(ROW + COL, None), check_vma=False
    )
```

```python
import functools

import jax
import jax.numpy as jnp
from jax import lax
from jax.experimental import pallas as pl
from jax.experimental.pallas import tpu as pltpu
from jax.sharding import Mesh, PartitionSpec as P

BF16 = jnp.bfloat16
F32 = jnp.float32
ROW = ("zlo", "y", "core")
CHIPS = ("zlo", "y")
COL = ("zhi", "x")
TILE_DOT = (((1,), (0,)), ((), ()))
TILE_T_DOT = (((0,), (0,)), ((), ()))
CUT = 256
SMEM = pl.BlockSpec(memory_space=pltpu.SMEM)
HBM = pl.BlockSpec(memory_space=pl.ANY)
VMEM = pl.BlockSpec(memory_space=pltpu.VMEM)


def clamp(sums, degree, known, label):
    classes = lax.broadcasted_iota(jnp.int32, sums.shape, 1)
    hot = (label[:, None] == classes).astype(F32)
    scaled = sums * lax.rsqrt(degree.astype(F32))[:, None]
    return jnp.where(known[:, None] == 1, hot, scaled).astype(BF16)


def add(*terms):
    total = terms[0].astype(F32)
    for term in terms[1:]:
        total = total + term.astype(F32)
    return total


def feature_kernel(
    table, tiles, pages, own, other, tile_buf, page_buf, acc, sems
):
    slots, edge, _ = tile_buf.shape
    half = edge // 2
    count = table[2 * slots]
    core = table[2 * slots + 3]

    def copies(slot):
        src = pl.multiple_of(table[slot] * edge, edge)
        return (
            pltpu.make_async_copy(tiles.at[slot], tile_buf.at[slot], sems.at[0, slot]),
            pltpu.make_async_copy(pages.at[pl.ds(src, edge)], page_buf.at[slot], sems.at[1, slot]),
        )

    @pl.loop(0, count)
    def _(slot):
        for copy in copies(slot):
            copy.start()

    acc[...] = jnp.zeros_like(acc)

    @pl.loop(0, count)
    def _(slot):
        for copy in copies(slot):
            copy.wait()
        acc[table[slots + slot]] += lax.dot_general(
            page_buf[slot], tile_buf[slot], TILE_T_DOT, preferred_element_type=F32
        )

    for low, high, here in ((own, other, 0), (other, own, 1)):

        @pl.when(core == here)
        def _():
            @pl.loop(0, acc.shape[0])
            def _(tile):
                low[tile] = acc[tile, :, :half].T
                high[tile] = acc[tile, :, half:].T


def feature_partials(table, tiles, pages, feats):
    slots, edge, _ = tiles.shape
    classes = pages.shape[1]
    halves = jax.ShapeDtypeStruct((feats // edge, edge // 2, classes), F32)
    return pl.pallas_call(
        feature_kernel,
        out_shape=[halves, halves],
        in_specs=[SMEM] + [HBM] * 2,
        out_specs=[VMEM] * 2,
        scratch_shapes=[
            pltpu.VMEM((slots, edge, edge), BF16),
            pltpu.VMEM((slots, edge, classes), BF16),
            pltpu.VMEM((feats // edge, classes, edge), F32),
            pltpu.SemaphoreType.DMA((2, slots)),
        ],
        compiler_params=pltpu.CompilerParams(vmem_limit_bytes=50 << 20),
        cost_estimate=pl.CostEstimate(
            flops=2 * slots * edge * edge * classes,
            bytes_accessed=2 * slots * edge * (edge + classes),
            transcendentals=0,
        ),
        name="feature_partials",
    )(table, tiles, pages)


def page_kernel(deltas, straight, per, table, tiles, mine, partner, *rest):
    n_out = 2 * len(deltas)
    outs, rest = rest[:n_out], rest[n_out:]
    if straight:
        first_out, rest = rest[0], rest[1:]
    tile_buf, feats, acc, head, nxt, sems, feat_sems = rest
    slots, edge, _ = tile_buf.shape
    half = edge // 2
    span = 4 * per
    page_tiles = head.shape[0]
    count = table[2 * slots]
    core = table[2 * slots + 3]

    def feature_copies():
        for which, source in ((core, mine), (1 - core, partner)):
            part = pl.ds(pl.multiple_of(which * half, half), half)
            yield pltpu.make_async_copy(source, feats.at[:, part], feat_sems.at[which])

    for copy in feature_copies():
        copy.start()

    @pl.loop(0, page_tiles, unroll=8)
    def _(r):
        head[r] = -1

    def tile_copy(slot):
        return pltpu.make_async_copy(tiles.at[slot], tile_buf.at[slot], sems.at[slot])

    @pl.loop(0, count)
    def _(slot):
        r = table[slot]
        owner, k = r // per, lax.rem(r, per)
        ahead = lax.rem(lax.rem(owner, 4) - table[2 * slots + 1] + 4, 4)
        r = ahead * span + lax.rem(owner // 4 - table[2 * slots + 2] + 4, 4) * per + k
        wanted = functools.reduce(jnp.logical_or, [ahead == d for d in deltas])
        if straight:
            wanted = jnp.logical_or(wanted, k == 0)

        @pl.when(wanted)
        def _():
            tile_copy(slot).start()
            nxt[slot] = head[r]
            head[r] = slot

    for out in outs:
        out[...] = jnp.zeros_like(out)
    if straight:
        first_out[...] = jnp.zeros_like(first_out)

    for copy in feature_copies():
        copy.wait()

    def product(slot):
        tile_copy(slot).wait()
        return lax.dot_general(
            tile_buf[slot], feats[table[slots + slot]], TILE_DOT, preferred_element_type=F32
        )

    def visit(delta, index, j):
        first = head[delta * span + index]
        second, k = index // per, lax.rem(index, per)

        @pl.when(first >= 0)
        def _():
            acc[...] = product(first)

            def body(slot):
                acc[...] += product(slot)
                return nxt[slot]

            lax.while_loop(lambda s: s >= 0, body, nxt[first])
            if straight:

                @pl.when(k == 0)
                def _():
                    slow = lax.rem(table[2 * slots + 2] + second, 4)
                    first_out[slow, delta] = acc[:CUT, :].astype(BF16)

            side = (edge - CUT) // 2
            for i in range(len(deltas)):
                even, odd = outs[2 * i], outs[2 * i + 1]

                @pl.when(jnp.logical_and(j == i, k == 0))
                def _():
                    even[second, pl.ds(edge, side)] = acc[CUT : CUT + side, :].astype(BF16)
                    odd[second, pl.ds(edge, side)] = acc[CUT + side :, :].astype(BF16)

                @pl.when(jnp.logical_and(j == i, k == 1))
                def _():
                    even[second, pl.ds(0, edge)] = acc[...].astype(BF16)

                @pl.when(jnp.logical_and(j == i, k == 2))
                def _():
                    odd[second, pl.ds(0, edge)] = acc[...].astype(BF16)

    others = [d for d in range(4) if d not in deltas] if straight else []
    walk = [(d, j, 1) for j, d in enumerate(deltas)] + [(d, -1, per) for d in others]

    @pl.loop(0, len(walk))
    def _(w):
        delta, j, step = [
            functools.reduce(
                lambda v, n: jnp.where(w == n, walk[n][f], v), range(1, len(walk)), jnp.int32(walk[0][f])
            )
            for f in range(3)
        ]

        @pl.loop(0, span // step)
        def _(i):
            visit(delta, i * step, j)


def page_partials(deltas, straight, table, tiles, mine, partner, page_tiles):
    slots, edge, _ = tiles.shape
    classes = mine.shape[-1]
    per = page_tiles // 16
    shapes = [(4, edge + (edge - CUT) // 2, classes)] * (2 * len(deltas))
    if straight:
        shapes.append((4, 4, CUT, classes))
    share = len(deltas) + (1 if straight else 0)
    out = pl.pallas_call(
        functools.partial(page_kernel, deltas, straight, per),
        out_shape=[jax.ShapeDtypeStruct(s, BF16) for s in shapes],
        in_specs=[SMEM] + [HBM] * 3,
        out_specs=[VMEM] * len(shapes),
        scratch_shapes=[
            pltpu.VMEM((slots, edge, edge), BF16),
            pltpu.VMEM((mine.shape[0], edge, classes), BF16),
            pltpu.VMEM((edge, classes), F32),
            pltpu.SMEM((page_tiles,), jnp.int32),
            pltpu.SMEM((slots,), jnp.int32),
            pltpu.SemaphoreType.DMA((slots,)),
            pltpu.SemaphoreType.DMA((2,)),
        ],
        compiler_params=pltpu.CompilerParams(vmem_limit_bytes=50 << 20),
        cost_estimate=pl.CostEstimate(
            flops=2 * slots * edge * edge * classes * share // 4,
            bytes_accessed=2 * slots * edge * edge * share // 4,
            transcendentals=0,
        ),
        name="page_partials",
    )(table, tiles, mine, partner)
    return [out[2 * i : 2 * i + 2] for i in range(len(deltas))], out[-1]


def shift(x, axis, by):
    return lax.ppermute(x, axis, [(i, (i + by) % 4) for i in range(4)])


def ring_terms(pieces, axis):
    far_up = shift(pieces[2][0], axis, 1)
    far_down = shift(pieces[2][1], axis, 3)
    near_up = shift(pieces[1][1], axis, 1)
    near_down = shift(pieces[3][0], axis, 3)
    up = shift(add(far_up, pieces[1][0]).astype(BF16), axis, 1)
    down = shift(add(far_down, pieces[3][1]).astype(BF16), axis, 3)
    return (pieces[0][0], near_down, up), (pieces[0][1], near_up, down)


def final_kernel(scale, base, s0, s1, s2, s3, a0, a1, a2, b0, b1, b2, out):
    edge = out.shape[0] // 3
    side = (edge - CUT) // 2

    def put(start, sums):
        rows = pl.ds(start, sums.shape[0])
        out[rows, :] = (sums * scale[rows, :] + base[rows, :].astype(F32)).astype(BF16)

    put(0, add(s0[...], s1[...], s2[...], s3[...]))
    for half, terms in ((0, (a0, a1, a2)), (1, (b0, b1, b2))):
        put(CUT + half * side, add(*[t[pl.ds(edge, side), :] for t in terms]))
        put((1 + half) * edge, add(*[t[pl.ds(0, edge), :] for t in terms]))


def split_kernel(a, b, c, *outs):
    for d in range(4):
        outs[d][...] = add(a[d], b[d], c[d]).astype(BF16)


def split_sums(*terms):
    piece = jax.ShapeDtypeStruct(terms[0].shape[1:], BF16)
    return pl.pallas_call(
        split_kernel,
        out_shape=[piece] * 4,
        in_specs=[VMEM] * 3,
        out_specs=[VMEM] * 4,
        compiler_params=pltpu.CompilerParams(vmem_limit_bytes=16 << 20),
        cost_estimate=pl.CostEstimate(
            flops=2 * terms[0].size, bytes_accessed=8 * terms[0].size, transcendentals=0
        ),
        name="split_sums",
    )(*terms)


def local(
    page_scores,
    tile_values,
    tile_row,
    tile_col,
    tile_count,
    page_seed,
    page_label,
    page_degree,
    feature_seed,
    feature_label,
    feature_degree,
):
    tiles = tile_values[0, 0]
    edge = tiles.shape[-1]
    half = edge // 2
    feats, classes = feature_seed.shape[0], page_scores.shape[1]
    page_tiles = page_scores.shape[0] // edge
    per = page_tiles // 16
    place = jnp.stack([lax.axis_index(a) for a in ("x", "zhi", "core")]).astype(jnp.int32)
    table = jnp.concatenate([tile_row[0, 0], tile_col[0, 0], tile_count[0], place])

    def swap(x):
        return lax.ppermute(x, "core", [(0, 1), (1, 0)])

    kept, other = feature_partials(table, tiles, page_scores, feats)
    pair = add(kept, swap(other)).astype(BF16)
    parts = lax.all_to_all(pair, CHIPS, 0, 0)
    first = lax.axis_index(ROW) * half

    def own(x):
        return lax.dynamic_slice_in_dim(x, first, half, 0)

    scores = clamp(
        parts.astype(F32).sum(0), own(feature_degree), own(feature_seed), own(feature_label)
    )
    mine = lax.all_to_all(jnp.broadcast_to(scores[None], pair.shape), CHIPS, 0, 0)
    partner = swap(mine)

    known = (page_seed == 1)[:, None]
    hot = page_label[:, None] == lax.broadcasted_iota(jnp.int32, (per * edge, classes), 1)
    base = jnp.where(jnp.logical_and(known, hot), 1.0, 0.0).astype(BF16)
    scale = jnp.where(known, 0.0, lax.rsqrt(page_degree.astype(F32))[:, None])
    scale = jnp.broadcast_to(scale, base.shape)

    def pages(deltas, straight, mine, partner):
        return page_partials(
            deltas, straight, table, tiles, mine, partner, page_tiles
        )

    (far,), _ = pages((2,), False, mine, partner)
    (ahead, behind), straight = pages((1, 3), True, mine, partner)
    straight = lax.all_to_all(straight, "zhi", 0, 0)
    far_up = shift(far[0], "x", 1)
    far_down = shift(far[1], "x", 3)
    near_up = shift(ahead[1], "x", 1)
    near_down = shift(behind[0], "x", 3)
    up = add(far_up, ahead[0]).astype(BF16)
    down = add(far_down, behind[1]).astype(BF16)
    up, down, mine, partner = lax.optimization_barrier((up, down, mine, partner))
    up = shift(up, "x", 1)
    down = shift(down, "x", 3)
    (here,), _ = pages((0,), False, mine, partner)
    base, scale, here = lax.optimization_barrier((base, scale, here))
    halves = [split_sums(here[0], near_down, up), split_sums(here[1], near_up, down)]
    straight = add(*[straight[i] for i in range(4)]).astype(BF16)
    straight = [straight[0]] + [shift(straight[d], "x", d) for d in (1, 3, 2)]
    even, odd = ring_terms([[h[d] for h in halves] for d in range(4)], "zhi")

    return pl.pallas_call(
        final_kernel,
        out_shape=jax.ShapeDtypeStruct(base.shape, BF16),
        in_specs=[VMEM] * 12,
        out_specs=VMEM,
        compiler_params=pltpu.CompilerParams(vmem_limit_bytes=16 << 20),
        name="final_sums",
    )(scale, base, *straight, *even, *odd)


def solution(mesh):
    parts = Mesh(mesh.devices.reshape(2, 4, 2, 4, 4), ROW + COL)
    in_specs = (
        P(ROW, None),
        P(ROW, COL, None, None, None),
        P(ROW, COL, None),
        P(ROW, COL, None),
        P(ROW, COL),
        P(ROW + COL),
        P(ROW + COL),
        P(ROW + COL),
        P(COL),
        P(COL),
        P(COL),
    )
    return jax.shard_map(
        local, mesh=parts, in_specs=in_specs, out_specs=P(ROW + COL, None), check_vma=False
    )
```

```python
import functools

import jax
import jax.numpy as jnp
from jax import lax
from jax.experimental import pallas as pl
from jax.experimental.pallas import tpu as pltpu
from jax.sharding import Mesh, PartitionSpec as P

BF16 = jnp.bfloat16
F32 = jnp.float32
ROW = ("zlo", "y", "core")
CHIPS = ("zlo", "y")
COL = ("zhi", "x")
TILE_DOT = (((1,), (0,)), ((), ()))
TILE_T_DOT = (((0,), (0,)), ((), ()))
CUT = 224
SMEM = pl.BlockSpec(memory_space=pltpu.SMEM)
HBM = pl.BlockSpec(memory_space=pl.ANY)
VMEM = pl.BlockSpec(memory_space=pltpu.VMEM)


def clamp(sums, degree, known, label):
    classes = lax.broadcasted_iota(jnp.int32, sums.shape, 1)
    hot = (label[:, None] == classes).astype(F32)
    scaled = sums * lax.rsqrt(degree.astype(F32))[:, None]
    return jnp.where(known[:, None] == 1, hot, scaled).astype(BF16)


def add(*terms):
    total = terms[0].astype(F32)
    for term in terms[1:]:
        total = total + term.astype(F32)
    return total


def feature_kernel(
    table, tiles, pages, own, other, tile_buf, page_buf, acc, sems
):
    slots, edge, _ = tile_buf.shape
    half = edge // 2
    count = table[2 * slots]
    core = table[2 * slots + 3]

    def copies(slot):
        src = pl.multiple_of(table[slot] * edge, edge)
        return (
            pltpu.make_async_copy(tiles.at[slot], tile_buf.at[slot], sems.at[0, slot]),
            pltpu.make_async_copy(pages.at[pl.ds(src, edge)], page_buf.at[slot], sems.at[1, slot]),
        )

    @pl.loop(0, count)
    def _(slot):
        for copy in copies(slot):
            copy.start()

    acc[...] = jnp.zeros_like(acc)

    @pl.loop(0, count)
    def _(slot):
        for copy in copies(slot):
            copy.wait()
        acc[table[slots + slot]] += lax.dot_general(
            page_buf[slot], tile_buf[slot], TILE_T_DOT, preferred_element_type=F32
        )

    for low, high, here in ((own, other, 0), (other, own, 1)):

        @pl.when(core == here)
        def _():
            @pl.loop(0, acc.shape[0])
            def _(tile):
                low[tile] = acc[tile, :, :half].T
                high[tile] = acc[tile, :, half:].T


def feature_partials(table, tiles, pages, feats):
    slots, edge, _ = tiles.shape
    classes = pages.shape[1]
    halves = jax.ShapeDtypeStruct((feats // edge, edge // 2, classes), F32)
    return pl.pallas_call(
        feature_kernel,
        out_shape=[halves, halves],
        in_specs=[SMEM] + [HBM] * 2,
        out_specs=[VMEM] * 2,
        scratch_shapes=[
            pltpu.VMEM((slots, edge, edge), BF16),
            pltpu.VMEM((slots, edge, classes), BF16),
            pltpu.VMEM((feats // edge, classes, edge), F32),
            pltpu.SemaphoreType.DMA((2, slots)),
        ],
        compiler_params=pltpu.CompilerParams(vmem_limit_bytes=50 << 20),
        cost_estimate=pl.CostEstimate(
            flops=2 * slots * edge * edge * classes,
            bytes_accessed=2 * slots * edge * (edge + classes),
            transcendentals=0,
        ),
        name="feature_partials",
    )(table, tiles, pages)


def page_kernel(deltas, straight, per, table, tiles, mine, partner, *rest):
    n_out = 2 * len(deltas)
    outs, rest = rest[:n_out], rest[n_out:]
    if straight:
        first_out, rest = rest[0], rest[1:]
    tile_buf, feats, acc, head, nxt, sems, feat_sems = rest
    slots, edge, _ = tile_buf.shape
    half = edge // 2
    span = 4 * per
    page_tiles = head.shape[0]
    count = table[2 * slots]
    core = table[2 * slots + 3]

    def feature_copies():
        for which, source in ((core, mine), (1 - core, partner)):
            part = pl.ds(pl.multiple_of(which * half, half), half)
            yield pltpu.make_async_copy(source, feats.at[:, part], feat_sems.at[which])

    for copy in feature_copies():
        copy.start()

    @pl.loop(0, page_tiles, unroll=8)
    def _(r):
        head[r] = -1

    def tile_copy(slot):
        return pltpu.make_async_copy(tiles.at[slot], tile_buf.at[slot], sems.at[slot])

    @pl.loop(0, count)
    def _(slot):
        r = table[slot]
        owner, k = r // per, lax.rem(r, per)
        ahead = lax.rem(lax.rem(owner, 4) - table[2 * slots + 1] + 4, 4)
        r = ahead * span + lax.rem(owner // 4 - table[2 * slots + 2] + 4, 4) * per + k
        wanted = functools.reduce(jnp.logical_or, [ahead == d for d in deltas])
        if straight:
            wanted = jnp.logical_or(wanted, k == 0)

        @pl.when(wanted)
        def _():
            tile_copy(slot).start()
            nxt[slot] = head[r]
            head[r] = slot

    for out in outs:
        out[...] = jnp.zeros_like(out)
    if straight:
        first_out[...] = jnp.zeros_like(first_out)

    for copy in feature_copies():
        copy.wait()

    def product(slot):
        tile_copy(slot).wait()
        return lax.dot_general(
            tile_buf[slot], feats[table[slots + slot]], TILE_DOT, preferred_element_type=F32
        )

    def visit(delta, index, j):
        first = head[delta * span + index]
        second, k = index // per, lax.rem(index, per)

        @pl.when(first >= 0)
        def _():
            acc[...] = product(first)

            def body(slot):
                acc[...] += product(slot)
                return nxt[slot]

            lax.while_loop(lambda s: s >= 0, body, nxt[first])
            if straight:

                @pl.when(k == 0)
                def _():
                    slow = lax.rem(table[2 * slots + 2] + second, 4)
                    first_out[slow, delta] = acc[:CUT, :].astype(BF16)

            side = (edge - CUT) // 2
            for i in range(len(deltas)):
                even, odd = outs[2 * i], outs[2 * i + 1]

                @pl.when(jnp.logical_and(j == i, k == 0))
                def _():
                    even[second, pl.ds(edge, side)] = acc[CUT : CUT + side, :].astype(BF16)
                    odd[second, pl.ds(edge, side)] = acc[CUT + side :, :].astype(BF16)

                @pl.when(jnp.logical_and(j == i, k == 1))
                def _():
                    even[second, pl.ds(0, edge)] = acc[...].astype(BF16)

                @pl.when(jnp.logical_and(j == i, k == 2))
                def _():
                    odd[second, pl.ds(0, edge)] = acc[...].astype(BF16)

    others = [d for d in range(4) if d not in deltas] if straight else []
    walk = [(d, j, 1) for j, d in enumerate(deltas)] + [(d, -1, per) for d in others]

    @pl.loop(0, len(walk))
    def _(w):
        delta, j, step = [
            functools.reduce(
                lambda v, n: jnp.where(w == n, walk[n][f], v), range(1, len(walk)), jnp.int32(walk[0][f])
            )
            for f in range(3)
        ]

        @pl.loop(0, span // step)
        def _(i):
            visit(delta, i * step, j)


def page_partials(deltas, straight, table, tiles, mine, partner, page_tiles):
    slots, edge, _ = tiles.shape
    classes = mine.shape[-1]
    per = page_tiles // 16
    shapes = [(4, edge + (edge - CUT) // 2, classes)] * (2 * len(deltas))
    if straight:
        shapes.append((4, 4, CUT, classes))
    share = len(deltas) + (1 if straight else 0)
    out = pl.pallas_call(
        functools.partial(page_kernel, deltas, straight, per),
        out_shape=[jax.ShapeDtypeStruct(s, BF16) for s in shapes],
        in_specs=[SMEM] + [HBM] * 3,
        out_specs=[VMEM] * len(shapes),
        scratch_shapes=[
            pltpu.VMEM((slots, edge, edge), BF16),
            pltpu.VMEM((mine.shape[0], edge, classes), BF16),
            pltpu.VMEM((edge, classes), F32),
            pltpu.SMEM((page_tiles,), jnp.int32),
            pltpu.SMEM((slots,), jnp.int32),
            pltpu.SemaphoreType.DMA((slots,)),
            pltpu.SemaphoreType.DMA((2,)),
        ],
        compiler_params=pltpu.CompilerParams(vmem_limit_bytes=50 << 20),
        cost_estimate=pl.CostEstimate(
            flops=2 * slots * edge * edge * classes * share // 4,
            bytes_accessed=2 * slots * edge * edge * share // 4,
            transcendentals=0,
        ),
        name="page_partials",
    )(table, tiles, mine, partner)
    return [out[2 * i : 2 * i + 2] for i in range(len(deltas))], out[-1]


def shift(x, axis, by):
    return lax.ppermute(x, axis, [(i, (i + by) % 4) for i in range(4)])


def ring_terms(pieces, axis):
    far_up = shift(pieces[2][0], axis, 1)
    far_down = shift(pieces[2][1], axis, 3)
    near_up = shift(pieces[1][1], axis, 1)
    near_down = shift(pieces[3][0], axis, 3)
    up = shift(add(far_up, pieces[1][0]).astype(BF16), axis, 1)
    down = shift(add(far_down, pieces[3][1]).astype(BF16), axis, 3)
    return (pieces[0][0], near_down, up), (pieces[0][1], near_up, down)


def final_kernel(scale, base, s0, s1, s2, s3, a0, a1, a2, b0, b1, b2, out):
    edge = out.shape[0] // 3
    side = (edge - CUT) // 2

    def put(start, sums):
        rows = pl.ds(start, sums.shape[0])
        out[rows, :] = (sums * scale[rows, :] + base[rows, :].astype(F32)).astype(BF16)

    put(0, add(s0[...], s1[...], s2[...], s3[...]))
    for half, terms in ((0, (a0, a1, a2)), (1, (b0, b1, b2))):
        put(CUT + half * side, add(*[t[pl.ds(edge, side), :] for t in terms]))
        put((1 + half) * edge, add(*[t[pl.ds(0, edge), :] for t in terms]))


def split_kernel(a, b, c, *outs):
    for d in range(4):
        outs[d][...] = add(a[d], b[d], c[d]).astype(BF16)


def split_sums(*terms):
    piece = jax.ShapeDtypeStruct(terms[0].shape[1:], BF16)
    return pl.pallas_call(
        split_kernel,
        out_shape=[piece] * 4,
        in_specs=[VMEM] * 3,
        out_specs=[VMEM] * 4,
        compiler_params=pltpu.CompilerParams(vmem_limit_bytes=16 << 20),
        cost_estimate=pl.CostEstimate(
            flops=2 * terms[0].size, bytes_accessed=8 * terms[0].size, transcendentals=0
        ),
        name="split_sums",
    )(*terms)


def local(
    page_scores,
    tile_values,
    tile_row,
    tile_col,
    tile_count,
    page_seed,
    page_label,
    page_degree,
    feature_seed,
    feature_label,
    feature_degree,
):
    tiles = tile_values[0, 0]
    edge = tiles.shape[-1]
    half = edge // 2
    feats, classes = feature_seed.shape[0], page_scores.shape[1]
    page_tiles = page_scores.shape[0] // edge
    per = page_tiles // 16
    place = jnp.stack([lax.axis_index(a) for a in ("x", "zhi", "core")]).astype(jnp.int32)
    table = jnp.concatenate([tile_row[0, 0], tile_col[0, 0], tile_count[0], place])

    def swap(x):
        return lax.ppermute(x, "core", [(0, 1), (1, 0)])

    kept, other = feature_partials(table, tiles, page_scores, feats)
    pair = add(kept, swap(other)).astype(BF16)
    parts = lax.all_to_all(pair, CHIPS, 0, 0)
    first = lax.axis_index(ROW) * half

    def own(x):
        return lax.dynamic_slice_in_dim(x, first, half, 0)

    scores = clamp(
        parts.astype(F32).sum(0), own(feature_degree), own(feature_seed), own(feature_label)
    )
    mine = lax.all_to_all(jnp.broadcast_to(scores[None], pair.shape), CHIPS, 0, 0)
    partner = swap(mine)

    known = (page_seed == 1)[:, None]
    hot = page_label[:, None] == lax.broadcasted_iota(jnp.int32, (per * edge, classes), 1)
    base = jnp.where(jnp.logical_and(known, hot), 1.0, 0.0).astype(BF16)
    scale = jnp.where(known, 0.0, lax.rsqrt(page_degree.astype(F32))[:, None])
    scale = jnp.broadcast_to(scale, base.shape)

    def pages(deltas, straight, mine, partner):
        return page_partials(
            deltas, straight, table, tiles, mine, partner, page_tiles
        )

    (far,), _ = pages((2,), False, mine, partner)
    (ahead, behind), straight = pages((1, 3), True, mine, partner)
    straight = lax.all_to_all(straight, "zhi", 0, 0)
    far_up = shift(far[0], "x", 1)
    far_down = shift(far[1], "x", 3)
    near_up = shift(ahead[1], "x", 1)
    near_down = shift(behind[0], "x", 3)
    up = add(far_up, ahead[0]).astype(BF16)
    down = add(far_down, behind[1]).astype(BF16)
    up, down, mine, partner = lax.optimization_barrier((up, down, mine, partner))
    up = shift(up, "x", 1)
    down = shift(down, "x", 3)
    (here,), _ = pages((0,), False, mine, partner)
    base, scale, here = lax.optimization_barrier((base, scale, here))
    halves = [split_sums(here[0], near_down, up), split_sums(here[1], near_up, down)]
    straight = add(*[straight[i] for i in range(4)]).astype(BF16)
    straight = [straight[0]] + [shift(straight[d], "x", d) for d in (1, 3, 2)]
    even, odd = ring_terms([[h[d] for h in halves] for d in range(4)], "zhi")

    return pl.pallas_call(
        final_kernel,
        out_shape=jax.ShapeDtypeStruct(base.shape, BF16),
        in_specs=[VMEM] * 12,
        out_specs=VMEM,
        compiler_params=pltpu.CompilerParams(vmem_limit_bytes=16 << 20),
        name="final_sums",
    )(scale, base, *straight, *even, *odd)


def solution(mesh):
    parts = Mesh(mesh.devices.reshape(2, 4, 2, 4, 4), ROW + COL)
    in_specs = (
        P(ROW, None),
        P(ROW, COL, None, None, None),
        P(ROW, COL, None),
        P(ROW, COL, None),
        P(ROW, COL),
        P(ROW + COL),
        P(ROW + COL),
        P(ROW + COL),
        P(COL),
        P(COL),
        P(COL),
    )
    return jax.shard_map(
        local, mesh=parts, in_specs=in_specs, out_specs=P(ROW + COL, None), check_vma=False
    )
```
